256 devices in a mesh: seq: 32 (over y, x, core), head: 8 (over z).
Axes of the slice: x: 4, y: 4, z: 8, core: 2. Of those that a mesh axis runs over, the one named last changes fastest.
Arguments:
- queries: bfloat16 [32768, 4096], P(('seq', 'head')), may hold values from -1.796875 to 1.796875
- keys: bfloat16 [32768, 4096], P(('seq', 'head')), may hold values from -1.796875 to 1.796875
- values: bfloat16 [32768, 4096], P(('seq', 'head')), may hold values from -1.796875 to 1.796875
- grad_out: bfloat16 [32768, 4096], P(('seq', 'head')), may hold values from -0.032958984 to 0.032958984
Outputs:
- grad_q: bfloat16 [32768, 4096], P(('seq', 'head'))
- grad_k: bfloat16 [32768, 4096], P(('seq', 'head'))
- grad_v: bfloat16 [32768, 4096], P(('seq', 'head'))
The draws below stay inside these ranges and needn't reach their ends.
All inputs are finite; a program needn't handle non-finite values.
Results may differ from the reference program's by a relative error of at most 0.0025.
Values may be sent and summed in bfloat16 or wider, within the bound.
No kernel may reach another device: no remote copies, remote signals or barrier semaphores. Data moves between devices by JAX's collectives and lax.ppermute only.
A program may use at most 128 MiB of HBM per device.

```python
import jax
import jax.numpy as jnp
from jax import lax

HEADS = 32
DK = 128
SPAN = 1024
SEQ = 32768
N_SEQ = 32


def levels(stream_key, shape, split, low, high):
    factor_of, own = 1.0, jax.random.fold_in(stream_key, 6)
    for dim, shards_of in split:
        steps = jnp.exp(jax.random.uniform(jax.random.fold_in(own, dim), (shards_of,), jnp.float32, low / len(split), high / len(split)))
        factor_of = factor_of * jnp.repeat(steps, shape[dim] // shards_of).reshape([-1 if axis == dim else 1 for axis in range(len(shape))])
    return factor_of


def normal_values(own_key, shape, deviation, limit, shards=(), dtype=jnp.bfloat16):
    level = levels(own_key, shape, shards, -0.22, 0.18) if shards else 1.0
    values = jax.random.normal(own_key, shape, jnp.float32) * deviation * level
    return jnp.minimum(jnp.maximum(values, -limit), limit).astype(dtype)


def setup_inputs(seed: int = 0) -> dict:
    splits = jax.random.split(jax.random.key(seed), 5)
    queries = normal_values(splits[0], (SEQ, HEADS * DK), 0.3, 1.796875, ((0, 256),))
    keys = normal_values(splits[1], (SEQ, HEADS * DK), 0.3, 1.796875, ((0, 256),))
    values = normal_values(splits[2], (SEQ, HEADS * DK), 0.3, 1.796875, ((0, 256),))
    grad_out = normal_values(splits[3], (SEQ, HEADS * DK), (SEQ ** -0.5), 0.032958984, ((0, 256),))
    return dict(queries=queries, keys=keys, values=values, grad_out=grad_out)


def one_head(block):
    query, key, value, grad = block
    qf = query.astype(jnp.float32)
    kf = key.astype(jnp.float32)
    vf = value.astype(jnp.float32)
    gf = grad.astype(jnp.float32)
    high = lax.Precision.HIGHEST
    key_state = jnp.einsum('ncd,nce->nde', kf, vf, precision=high)
    grad_state = jnp.einsum('ncd,nce->nde', qf, gf, precision=high)
    prefix = jnp.cumsum(key_state, axis=0) - key_state
    suffix = jnp.sum(grad_state, axis=0)[None] - jnp.cumsum(grad_state, axis=0)
    position = lax.iota(jnp.int32, SPAN)
    causal = position[:, None] >= position[None, :]
    weights_a = jnp.where(causal[None], jnp.einsum('nte,nse->nts', gf, vf, precision=high), 0.0).astype(jnp.bfloat16).astype(jnp.float32)
    weights_b = jnp.where(causal[None], jnp.einsum('ntd,nsd->nts', qf, kf, precision=high), 0.0).astype(jnp.bfloat16).astype(jnp.float32)
    grad_query = jnp.einsum('nts,nsd->ntd', weights_a, kf, precision=high) + jnp.einsum('nte,nde->ntd', gf, prefix, precision=high)
    grad_key = jnp.einsum('nts,ntd->nsd', weights_a, qf, precision=high) + jnp.einsum('nse,nde->nsd', vf, suffix, precision=high)
    grad_value = jnp.einsum('nts,ntd->nsd', weights_b, gf, precision=high) + jnp.einsum('nsd,nde->nse', kf, suffix, precision=high)
    return (grad_query.astype(jnp.bfloat16), grad_key.astype(jnp.bfloat16), grad_value.astype(jnp.bfloat16))


def split_heads(array):
    return jnp.transpose(array.reshape(N_SEQ, SPAN, HEADS, DK), (2, 0, 1, 3))


def join_heads(array):
    return jnp.transpose(array, (1, 2, 0, 3)).reshape(N_SEQ * SPAN, HEADS * DK)


def reference(queries, keys, values, grad_out):
    blocks = (split_heads(queries), split_heads(keys), split_heads(values), split_heads(grad_out))
    grad_query, grad_key, grad_value = lax.map(one_head, blocks)
    return (join_heads(grad_query), join_heads(grad_key), join_heads(grad_value))
```

```python
import jax
import jax.numpy as jnp
from jax import lax
from jax.experimental import pallas as pl
from jax.experimental.pallas import tpu as pltpu
from jax.sharding import PartitionSpec as P

DK = 128
BLOCK = 256
GROUPS = 2
MIB = 1 << 20


VMEM = pl.BlockSpec(memory_space=pltpu.VMEM)
ANY = pl.BlockSpec(memory_space=pl.ANY)


def nt(a, b):
    return lax.dot_general(a, b, (((1,), (1,)), ((), ())), preferred_element_type=jnp.float32)


def nn(a, b):
    return lax.dot_general(a, b, (((1,), (0,)), ((), ())), preferred_element_type=jnp.float32)


def tn(a, b):
    return lax.dot_general(a, b, (((0,), (0,)), ((), ())), preferred_element_type=jnp.float32)


def split_parts(arrays, group, size, width):
    tokens = arrays[0].shape[0]
    per_dest = arrays[0].shape[1] // size
    count = len(arrays)

    def kernel(*refs):
        ins, outs, sem = refs[:count], refs[count:-1], refs[-1]
        mine = lax.axis_index("head")
        copies = []
        for distance in range(size):
            dest = lax.rem(mine + distance, size)
            start = pl.multiple_of(dest * per_dest + group * width, width)
            for which in range(count):
                copies.append(
                    pltpu.make_async_copy(
                        ins[which].at[:, pl.ds(start, width)],
                        outs[distance].at[which],
                        sem.at[distance, which],
                    )
                )
        for copy in copies:
            copy.start()
        for copy in copies:
            copy.wait()

    return pl.pallas_call(
        kernel,
        out_shape=[jax.ShapeDtypeStruct((count, tokens, width), arrays[0].dtype)] * size,
        in_specs=[ANY] * count,
        out_specs=[VMEM] * size,
        scratch_shapes=[pltpu.SemaphoreType.DMA((size, count))],
        compiler_params=pltpu.CompilerParams(vmem_limit_bytes=16 * MIB),
        cost_estimate=pl.CostEstimate(flops=0, transcendentals=0, bytes_accessed=8 * count * tokens * width * 2),
        name="split_parts",
    )(*arrays)


def exchange(parts, size):
    got = [parts[0]]
    for distance in range(1, size):
        pairs = [(i, (i + distance) % size) for i in range(size)]
        got.append(lax.ppermute(parts[distance], "head", pairs))
    return got


def span_states(parts, size, pieces):
    count, tokens, width = parts[0].shape
    heads = width // DK
    rows = heads * DK // pieces

    def kernel(*refs):
        ins, (x_ref, state_ref) = refs[:size], refs[size:]
        mine = lax.axis_index("head")
        for distance in range(size):
            source = lax.rem(mine + size - distance, size)
            at = pl.multiple_of(source * tokens, tokens)
            for which in range(count):
                x_ref[which, pl.ds(at, tokens), :] = ins[distance][which]
        for head in range(heads):
            cols = slice(head * DK, (head + 1) * DK)
            places = slice(head * pieces // heads, (head + 1) * pieces // heads)
            key_state = tn(x_ref[1, :, cols], x_ref[2, :, cols])
            state_ref[places, :rows, :] = key_state.reshape(pieces // heads, rows, DK)
            grad_state = tn(x_ref[0, :, cols], x_ref[3, :, cols])
            state_ref[places, rows:, :] = grad_state.reshape(pieces // heads, rows, DK)

    return pl.pallas_call(
        kernel,
        out_shape=[
            jax.ShapeDtypeStruct((count, size * tokens, width), parts[0].dtype),
            jax.ShapeDtypeStruct((pieces, 2 * rows, DK), jnp.float32),
        ],
        in_specs=[VMEM] * size,
        out_specs=[VMEM, VMEM],
        compiler_params=pltpu.CompilerParams(vmem_limit_bytes=24 * MIB),
        cost_estimate=pl.CostEstimate(
            flops=4 * size * tokens * width * DK, transcendentals=0, bytes_accessed=2 * count * size * tokens * width * 2
        ),
        name="span_states",
    )(*parts)


def running(states):
    pieces, both, width = states.shape
    rows = both // 2

    def kernel(in_ref, out_ref):
        total = jnp.zeros((rows, width), jnp.float32)
        for n in range(pieces):
            out_ref[n, :rows, :] = total
            total = total + in_ref[n, :rows, :]
        total = jnp.zeros((rows, width), jnp.float32)
        for n in reversed(range(pieces)):
            out_ref[n, rows:, :] = total
            total = total + in_ref[n, rows:, :]

    return pl.pallas_call(
        kernel,
        out_shape=jax.ShapeDtypeStruct(states.shape, jnp.float32),
        in_specs=[VMEM],
        out_specs=VMEM,
        compiler_params=pltpu.CompilerParams(vmem_limit_bytes=4 * MIB),
        name="running",
    )(states)


def halves(value):
    high = value.astype(jnp.bfloat16)
    low = (value - high.astype(jnp.float32)).astype(jnp.bfloat16)
    return high, low


def span_grads(x, carried, size):
    count, span, width = x.shape
    heads = width // DK
    tokens = span // size
    pieces, both, _ = carried.shape
    rows = both // 2
    blocks = span // BLOCK

    def kernel(*refs):
        x_ref, carried_ref = refs[:2]
        outs, (acc_ref, out_ref) = refs[2 : 2 + size], refs[2 + size :]
        mine = lax.axis_index("head")
        row = lax.broadcasted_iota(jnp.int32, (BLOCK, BLOCK), 0)
        col = lax.broadcasted_iota(jnp.int32, (BLOCK, BLOCK), 1)
        lower = row >= col
        upper = row <= col
        for head in range(heads):
            cols = slice(head * DK, (head + 1) * DK)
            places = slice(head * pieces // heads, (head + 1) * pieces // heads)
            prefix_high, prefix_low = halves(carried_ref[places, :rows, :].reshape(DK, DK))
            suffix_high, suffix_low = halves(carried_ref[places, rows:, :].reshape(DK, DK))
            for at in range(blocks):
                here = slice(at * BLOCK, (at + 1) * BLOCK)
                query, key = x_ref[0, here, cols], x_ref[1, here, cols]
                value, grad = x_ref[2, here, cols], x_ref[3, here, cols]
                total = nt(grad, prefix_high) + nt(grad, prefix_low)
                for other in range(at + 1):
                    there = slice(other * BLOCK, (other + 1) * BLOCK)
                    weights = nt(grad, x_ref[2, there, cols])
                    if other == at:
                        weights = jnp.where(lower, weights, 0.0)
                    total = total + nn(weights.astype(jnp.bfloat16), x_ref[1, there, cols])
                out_ref[0, here, cols] = total.astype(jnp.bfloat16)
                key_total = nt(value, suffix_high) + nt(value, suffix_low)
                value_total = nn(key, suffix_high) + nn(key, suffix_low)
                for other in range(at, blocks):
                    there = slice(other * BLOCK, (other + 1) * BLOCK)
                    weights_a = nt(value, x_ref[3, there, cols])
                    weights_b = nt(key, x_ref[0, there, cols])
                    if other == at:
                        weights_a = jnp.where(upper, weights_a, 0.0)
                        weights_b = jnp.where(upper, weights_b, 0.0)
                    key_total = key_total + nn(weights_a.astype(jnp.bfloat16), x_ref[0, there, cols])
                    value_total = value_total + nn(weights_b.astype(jnp.bfloat16), x_ref[3, there, cols])
                out_ref[1, here, cols] = key_total.astype(jnp.bfloat16)
                out_ref[2, here, cols] = value_total.astype(jnp.bfloat16)
        for distance in range(size):
            dest = lax.rem(mine + distance, size)
            at = pl.multiple_of(dest * tokens, tokens)
            for which in range(3):
                outs[distance][which] = out_ref[which, pl.ds(at, tokens), :]

    return pl.pallas_call(
        kernel,
        out_shape=[jax.ShapeDtypeStruct((3, tokens, width), x.dtype)] * size,
        in_specs=[VMEM, VMEM],
        out_specs=[VMEM] * size,
        scratch_shapes=[pltpu.VMEM((8, DK), jnp.float32), pltpu.VMEM((3, span, width), x.dtype)],
        compiler_params=pltpu.CompilerParams(vmem_limit_bytes=24 * MIB),
        cost_estimate=pl.CostEstimate(
            flops=8 * span * span * width, transcendentals=0, bytes_accessed=7 * span * width * 2
        ),
        name="span_grads",
    )(x, carried)


def join_parts(groups, size, width):
    _, tokens, _ = groups[0][0].shape
    count = len(groups)
    full = size * count * width

    def kernel(*refs):
        ins, outs, sem = refs[: count * size], refs[count * size : -1], refs[-1]
        mine = lax.axis_index("head")
        copies = []
        for group in range(count):
            for distance in range(size):
                source = lax.rem(mine + size - distance, size)
                start = pl.multiple_of(source * count * width + group * width, width)
                for which in range(3):
                    copies.append(
                        pltpu.make_async_copy(
                            ins[group * size + distance].at[which],
                            outs[which].at[:, pl.ds(start, width)],
                            sem.at[group * size + distance, which],
                        )
                    )
        for copy in copies:
            copy.start()
        for copy in copies:
            copy.wait()

    return pl.pallas_call(
        kernel,
        out_shape=[jax.ShapeDtypeStruct((tokens, full), groups[0][0].dtype)] * 3,
        in_specs=[VMEM] * (count * size),
        out_specs=[ANY] * 3,
        scratch_shapes=[pltpu.SemaphoreType.DMA((count * size, 3))],
        compiler_params=pltpu.CompilerParams(vmem_limit_bytes=16 * MIB),
        name="join_parts",
    )(*[part for group in groups for part in group])


def body(queries, keys, values, grad_out):
    size, spans = lax.axis_size("head"), lax.axis_size("seq")
    width = queries.shape[1] // size // GROUPS
    arrays = (queries, keys, values, grad_out)
    results = []
    for group in range(GROUPS):
        with jax.named_scope(f"group{group}"):
            parts = split_parts(arrays, group, size, width)
            with jax.named_scope("enter"):
                parts = exchange(parts, size)
            x, states = span_states(parts, size, spans)
            with jax.named_scope("scan"):
                states = lax.all_to_all(states, "seq", 0, 0, tiled=True)
                carried = lax.all_to_all(running(states), "seq", 0, 0, tiled=True)
            parts = span_grads(x, carried, size)
            with jax.named_scope("leave"):
                results.append(exchange(parts, size))
    return tuple(join_parts(results, size, width))


def solution(mesh):
    spec = P(("seq", "head"), None)
    return jax.shard_map(body, mesh=mesh, in_specs=(spec,) * 4, out_specs=(spec,) * 3, check_vma=False)
```

```python
import jax
import jax.numpy as jnp
from jax import lax
from jax.experimental import pallas as pl
from jax.experimental.pallas import tpu as pltpu
from jax.sharding import PartitionSpec as P


DK = 128
BLOCK = 256
GROUPS = 2
MIB = 1 << 20


VMEM = pl.BlockSpec(memory_space=pltpu.VMEM)
HBM = pl.BlockSpec(memory_space=pltpu.HBM)


def in_hbm(array):
    return pltpu.with_memory_space_constraint(array, pltpu.HBM)


def nt(a, b):
    return lax.dot_general(a, b, (((1,), (1,)), ((), ())), preferred_element_type=jnp.float32)


def nn(a, b):
    return lax.dot_general(a, b, (((1,), (0,)), ((), ())), preferred_element_type=jnp.float32)


def tn(a, b):
    return lax.dot_general(a, b, (((0,), (0,)), ((), ())), preferred_element_type=jnp.float32)


def split_parts(arrays, group, size, width):
    tokens = arrays[0].shape[0]
    per_dest = arrays[0].shape[1] // size
    count = len(arrays)

    def kernel(*refs):
        ins, outs, sem = refs[:count], refs[count:-1], refs[-1]
        mine = lax.axis_index("head")
        copies = []
        for distance in range(size):
            dest = lax.rem(mine + distance, size)
            start = pl.multiple_of(dest * per_dest + group * width, width)
            for which in range(count):
                copies.append(
                    pltpu.make_async_copy(
                        ins[which].at[:, pl.ds(start, width)],
                        outs[distance].at[which],
                        sem.at[distance, which],
                    )
                )
        for copy in copies:
            copy.start()
        for copy in copies:
            copy.wait()

    return pl.pallas_call(
        kernel,
        out_shape=[jax.ShapeDtypeStruct((count, tokens, width), arrays[0].dtype)] * size,
        in_specs=[HBM] * count,
        out_specs=[VMEM] * size,
        scratch_shapes=[pltpu.SemaphoreType.DMA((size, count))],
        compiler_params=pltpu.CompilerParams(vmem_limit_bytes=16 * MIB),
        cost_estimate=pl.CostEstimate(flops=0, transcendentals=0, bytes_accessed=8 * count * tokens * width * 2),
        name="split_parts",
    )(*[in_hbm(array) for array in arrays])


def distances(size):
    return sorted(range(1, size), key=lambda d: (-min(d, size - d), d))


def exchange(parts, size):
    got = list(parts)
    for distance in distances(size):
        pairs = [(i, (i + distance) % size) for i in range(size)]
        got[distance] = lax.ppermute(parts[distance], "head", pairs)
    return got


def span_states(parts, size, pieces):
    count, tokens, width = parts[0].shape
    heads = width // DK
    rows = heads * DK // pieces

    def kernel(*refs):
        ins, (out_ref, state_ref, x_ref, sem) = refs[:size], refs[size:]
        mine = lax.axis_index("head")
        for distance in range(size):
            source = lax.rem(mine + size - distance, size)
            at = pl.multiple_of(source * tokens, tokens)
            for which in range(count):
                x_ref[which, pl.ds(at, tokens), :] = ins[distance][which]
        keep = pltpu.make_async_copy(x_ref, out_ref, sem)
        keep.start()
        for head in range(heads):
            cols = slice(head * DK, (head + 1) * DK)
            places = slice(head * pieces // heads, (head + 1) * pieces // heads)
            key_state = tn(x_ref[1, :, cols], x_ref[2, :, cols])
            state_ref[places, :rows, :] = key_state.reshape(pieces // heads, rows, DK)
            grad_state = tn(x_ref[0, :, cols], x_ref[3, :, cols])
            state_ref[places, rows:, :] = grad_state.reshape(pieces // heads, rows, DK)
        keep.wait()

    return pl.pallas_call(
        kernel,
        out_shape=[
            pltpu.HBM((count, size * tokens, width), parts[0].dtype),
            jax.ShapeDtypeStruct((pieces, 2 * rows, DK), jnp.float32),
        ],
        in_specs=[VMEM] * size,
        out_specs=[HBM, VMEM],
        scratch_shapes=[pltpu.VMEM((count, size * tokens, width), parts[0].dtype), pltpu.SemaphoreType.DMA],
        compiler_params=pltpu.CompilerParams(vmem_limit_bytes=16 * MIB),
        cost_estimate=pl.CostEstimate(
            flops=4 * size * tokens * width * DK, transcendentals=0, bytes_accessed=2 * count * size * tokens * width * 2
        ),
        name="span_states",
    )(*parts)


def running(states):
    pieces, both, width = states.shape
    rows = both // 2

    def kernel(in_ref, out_ref):
        total = jnp.zeros((rows, width), jnp.float32)
        for n in range(pieces):
            out_ref[n, :rows, :] = total
            total = total + in_ref[n, :rows, :]
        total = jnp.zeros((rows, width), jnp.float32)
        for n in reversed(range(pieces)):
            out_ref[n, rows:, :] = total
            total = total + in_ref[n, rows:, :]

    return pl.pallas_call(
        kernel,
        out_shape=jax.ShapeDtypeStruct(states.shape, jnp.float32),
        in_specs=[VMEM],
        out_specs=VMEM,
        compiler_params=pltpu.CompilerParams(vmem_limit_bytes=4 * MIB),
        name="running",
    )(states)


def halves(value):
    high = value.astype(jnp.bfloat16)
    low = (value - high.astype(jnp.float32)).astype(jnp.bfloat16)
    return high, low


def span_grads(x, carried, size):
    count, span, width = x.shape
    heads = width // DK
    tokens = span // size
    pieces, both, _ = carried.shape
    rows = both // 2
    blocks = span // BLOCK

    def kernel(*refs):
        held_ref, carried_ref = refs[:2]
        outs, (x_ref, out_ref, sem) = refs[2 : 2 + size], refs[2 + size :]
        fetch = pltpu.make_async_copy(held_ref, x_ref, sem)
        fetch.start()
        mine = lax.axis_index("head")
        row = lax.broadcasted_iota(jnp.int32, (BLOCK, BLOCK), 0)
        col = lax.broadcasted_iota(jnp.int32, (BLOCK, BLOCK), 1)
        lower = row >= col
        upper = row <= col
        fetch.wait()

        @pl.loop(0, heads)
        def _(head):
            cols = pl.ds(pl.multiple_of(head * DK, DK), DK)
            places = pl.ds(head * (pieces // heads), pieces // heads)
            prefix_high, prefix_low = halves(carried_ref[places, :rows, :].reshape(DK, DK))
            suffix_high, suffix_low = halves(carried_ref[places, rows:, :].reshape(DK, DK))
            for at in range(blocks):
                here = slice(at * BLOCK, (at + 1) * BLOCK)
                key = x_ref[1, here, cols]
                value, grad = x_ref[2, here, cols], x_ref[3, here, cols]
                total = nt(grad, prefix_high) + nt(grad, prefix_low)
                for other in range(at + 1):
                    there = slice(other * BLOCK, (other + 1) * BLOCK)
                    weights = nt(grad, x_ref[2, there, cols])
                    if other == at:
                        weights = jnp.where(lower, weights, 0.0)
                    total = total + nn(weights.astype(jnp.bfloat16), x_ref[1, there, cols])
                out_ref[0, here, cols] = total.astype(jnp.bfloat16)
                key_total = nt(value, suffix_high) + nt(value, suffix_low)
                value_total = nn(key, suffix_high) + nn(key, suffix_low)
                for other in range(at, blocks):
                    there = slice(other * BLOCK, (other + 1) * BLOCK)
                    weights_a = nt(value, x_ref[3, there, cols])
                    weights_b = nt(key, x_ref[0, there, cols])
                    if other == at:
                        weights_a = jnp.where(upper, weights_a, 0.0)
                        weights_b = jnp.where(upper, weights_b, 0.0)
                    key_total = key_total + nn(weights_a.astype(jnp.bfloat16), x_ref[0, there, cols])
                    value_total = value_total + nn(weights_b.astype(jnp.bfloat16), x_ref[3, there, cols])
                out_ref[1, here, cols] = key_total.astype(jnp.bfloat16)
                out_ref[2, here, cols] = value_total.astype(jnp.bfloat16)

        for distance in range(size):
            dest = lax.rem(mine + distance, size)
            at = pl.multiple_of(dest * tokens, tokens)
            for which in range(3):
                outs[distance][which] = out_ref[which, pl.ds(at, tokens), :]

    return pl.pallas_call(
        kernel,
        out_shape=[jax.ShapeDtypeStruct((3, tokens, width), x.dtype)] * size,
        in_specs=[HBM, VMEM],
        out_specs=[VMEM] * size,
        scratch_shapes=[
            pltpu.VMEM((count, span, width), x.dtype),
            pltpu.VMEM((3, span, width), x.dtype),
            pltpu.SemaphoreType.DMA,
        ],
        compiler_params=pltpu.CompilerParams(vmem_limit_bytes=16 * MIB),
        cost_estimate=pl.CostEstimate(
            flops=8 * span * span * width, transcendentals=0, bytes_accessed=7 * span * width * 2
        ),
        name="span_grads",
    )(in_hbm(x), carried)


def join_parts(groups, size, width):
    _, tokens, _ = groups[0][0].shape
    count = len(groups)
    full = size * count * width

    def kernel(*refs):
        ins, outs, sem = refs[: count * size], refs[count * size : -1], refs[-1]
        mine = lax.axis_index("head")
        copies = []
        for group in range(count):
            for distance in range(size):
                source = lax.rem(mine + size - distance, size)
                start = pl.multiple_of(source * count * width + group * width, width)
                for which in range(3):
                    copies.append(
                        pltpu.make_async_copy(
                            ins[group * size + distance].at[which],
                            outs[which].at[:, pl.ds(start, width)],
                            sem.at[group * size + distance, which],
                        )
                    )
        for copy in copies:
            copy.start()
        for copy in copies:
            copy.wait()

    return pl.pallas_call(
        kernel,
        out_shape=[jax.ShapeDtypeStruct((tokens, full), groups[0][0].dtype)] * 3,
        in_specs=[VMEM] * (count * size),
        out_specs=[HBM] * 3,
        scratch_shapes=[pltpu.SemaphoreType.DMA((count * size, 3))],
        compiler_params=pltpu.CompilerParams(vmem_limit_bytes=16 * MIB),
        name="join_parts",
    )(*[part for group in groups for part in group])


def body(queries, keys, values, grad_out):
    size, spans = lax.axis_size("head"), lax.axis_size("seq")
    width = queries.shape[1] // size // GROUPS
    arrays = (queries, keys, values, grad_out)
    entered = []
    for group in range(GROUPS):
        parts = split_parts(arrays, group, size, width)
        if entered:
            entered[-1][3], parts = lax.optimization_barrier((entered[-1][3], parts))
        entered.append(exchange(parts, size))
    results, sent = [], None
    for group in range(GROUPS):
        parts = entered[group]
        if sent is not None:
            results.append(exchange(sent, size))
            parts, _ = lax.optimization_barrier((parts, sent))
        x, states = span_states(parts, size, spans)
        states = lax.all_to_all(states, "seq", 0, 0, tiled=True)
        carried = lax.all_to_all(running(states), "seq", 0, 0, tiled=True)
        sent = span_grads(x, carried, size)
    results.append(exchange(sent, size))
    return tuple(join_parts(results, size, width))


def solution(mesh):
    spec = P(("seq", "head"), None)
    return jax.shard_map(body, mesh=mesh, in_specs=(spec,) * 4, out_specs=(spec,) * 3, check_vma=False)
```
